32 devices in a mesh: chain: 2 (over y), px: 8 (over z, x), py: 2 (over core).
Axes of the slice: x: 2, y: 2, z: 4, core: 2. Of those that a mesh axis runs over, the one named last changes fastest.
Arguments:
- adjoint: float32 [512, 256, 256], P(('chain', 'px'), 'py'), parts along dimension 0, may hold values from -6 to 6
- saved: float32 [512, 256, 256], P(('chain', 'px'), 'py'), parts along dimension 0, may hold values from -6 to 6
- spectra: bfloat16 [2, 256, 256, 256], P(None, None, 'px'), may hold values from -6 to 6, as said below
- freq_index: int32 [8], replicated, may hold values from 1 to 8
- picked: int32 [2], replicated, may hold values from 0 to 7
Outputs:
- force: float32 [512, 256, 256], P(('chain', 'px'), 'py'), parts along dimension 0
The draws below stay inside these ranges and needn't reach their ends.
There are 2 independent parts, one for each index of `chain`. The reference program is written for one: setup_inputs(seed, part) draws one part's arguments, and reference() takes and returns one part's arrays. A program takes and returns all parts, laid end to end along the dimension named above; an argument that names none is the same for every part. Nothing has to cross between parts.
Inputs may be any that keep to these rules, and one draw needn't show every extreme that they name: Each kernel is even in every momentum coordinate separately: spectra[j][k1, k2, k3] is unchanged when k1 is replaced by (256 - k1) mod 256, and likewise k2 with 256 and k3 with 256.
All inputs are finite; a program needn't handle non-finite values.
Results may differ from the reference program's by a relative error of at most 0.0003.
Values sent between devices are 32-bit elements; how exact they have to be, the bound alone decides.
A program may use at most 128 MiB of HBM per device.

```python
import math
import jax
import jax.numpy as jnp

L1 = 256
L2 = 256
L3 = 256
FEATS = 8
WINDOW = 2


def folded_index(length):
    counter = jnp.arange(length, dtype=jnp.int32)
    return jnp.minimum(counter, length - counter).astype(jnp.int32)


def draw_spectra(key, part):
    reduced = jax.random.normal(key, (WINDOW, L1 // 2 + 1, L2 // 2 + 1, L3 // 2 + 1), jnp.float32)
    reduced = jnp.clip(reduced, -6.0, 6.0)
    expanded = jnp.take(reduced, folded_index(L1), axis=1)
    expanded = jnp.take(expanded, folded_index(L2), axis=2)
    expanded = jnp.take(expanded, folded_index(L3), axis=3)
    return expanded.astype(jnp.bfloat16)


def set_ends(drawn, own_key, low, largest):
    extent = drawn.shape
    index_at = [jax.random.randint(jax.random.fold_in(own_key, axis), (), 0, extent[axis]) for axis in range(len(extent))]
    drawn = drawn.at[tuple(index_at)].set(low)
    longest = extent.index(max(extent))
    index_at[longest] = (index_at[longest] + 1) % extent[longest]
    return drawn.at[tuple(index_at)].set(largest)


def levels(key, shape, shards, smallest, largest):
    factor_of = 1.0
    for position, parts in shards:
        heights = jax.random.uniform(jax.random.fold_in(jax.random.fold_in(key, 6), position), (parts,), jnp.float32, smallest / len(shards), largest / len(shards))
        factor_of = factor_of * jnp.repeat(jnp.exp(heights), shape[position] // parts).reshape((-1,) + (1,) * (len(shape) - 1 - position))
    return factor_of


def scatter_about(rng, dims, scale, reach, shards=(), held_as=jnp.bfloat16):
    gain = levels(rng, dims, shards, -0.22, 0.18) if shards else 1.0
    values = jax.random.normal(rng, dims, jnp.float32) * scale * gain
    return jnp.minimum(jnp.maximum(values, -reach), reach).astype(held_as)


def setup_inputs(seed: int = 0, part: int = 0) -> dict:
    arg_keys = jax.random.split(jax.random.key(seed), 6)
    part_splits = jax.random.split(jax.random.fold_in(arg_keys[5], part), 6)
    return {
        "adjoint": scatter_about(part_splits[0], (L1, L2, L3), 1.0, 6.0, ((0, 8), (1, 2)), jnp.float32),
        "saved": scatter_about(part_splits[1], (L1, L2, L3), 1.0, 6.0, ((0, 8), (1, 2)), jnp.float32),
        "spectra": draw_spectra(jax.random.fold_in(arg_keys[5], 71), part),
        "freq_index": set_ends(jax.random.randint(arg_keys[3], (FEATS,), 1, 9), jax.random.fold_in(arg_keys[3], 1), 1, 8).astype(jnp.int32),
        "picked": jax.random.randint(arg_keys[4], (WINDOW,), 0, FEATS).astype(jnp.int32),
    }


def reference(adjoint, saved, spectra, freq_index, picked):
    spectrum = jnp.fft.fftn(adjoint)
    total = jnp.zeros(adjoint.shape, jnp.float32)
    for slot in range(WINDOW):
        omega = (math.pi / 8.0) * freq_index[picked[slot]].astype(jnp.float32)
        field = jnp.real(jnp.fft.ifftn(spectra[slot].astype(jnp.float32) * spectrum))
        total = total + omega * jnp.cos(omega * saved) * field
    return total
```

```python
import functools
import math

import jax
import jax.numpy as jnp
import numpy as np
from jax import lax
from jax.experimental import pallas as pl
from jax.experimental.pallas import tpu as pltpu
from jax.sharding import PartitionSpec as P


def hartley(length):
    counter = np.arange(length, dtype=np.int64)
    angle = (counter[:, None] * counter[None, :] % length) * (2.0 * np.pi / length)
    return np.cos(angle) + np.sin(angle)


def chosen_index(freq_index, picked):
    ids = jnp.arange(freq_index.shape[0], dtype=jnp.int32)
    return jnp.sum(jnp.where(ids[None, :] == picked[:, None], freq_index[None, :], 0), axis=1)


def along(equation, field, table):
    return jnp.einsum(equation, field, jnp.asarray(table, jnp.float32), precision=lax.Precision.HIGH)


def plain_path(adjoint, saved, spectra, chosen):
    size_px, size_py = lax.axis_size("px"), lax.axis_size("py")
    one, two, three = adjoint.shape[0] * size_px, adjoint.shape[1] * size_py, adjoint.shape[2]
    t_one, t_two, t_three = hartley(one), hartley(two), hartley(three)
    width = three // size_py
    field = along("abc,cz->abz", adjoint, t_three)
    field = lax.all_to_all(field, "py", split_axis=2, concat_axis=1, tiled=True)
    field = along("abc,bz->azc", field, t_two)
    field = lax.all_to_all(field, "px", split_axis=1, concat_axis=0, tiled=True)
    spectrum = along("abc,az->zbc", field, t_one)
    kernels = lax.dynamic_slice_in_dim(spectra, lax.axis_index("py") * width, width, 3)
    omegas = chosen.astype(jnp.float32) * (math.pi / 8.0)
    scale = 1.0 / (one * two * three)
    total = jnp.zeros(saved.shape, jnp.float32)
    for slot in range(chosen.shape[0]):
        back = along("abc,az->zbc", spectrum * kernels[slot].astype(jnp.float32), t_one)
        back = lax.all_to_all(back, "px", split_axis=0, concat_axis=1, tiled=True)
        back = along("abc,bz->azc", back, t_two)
        back = lax.all_to_all(back, "py", split_axis=1, concat_axis=2, tiled=True)
        back = along("abc,cz->abz", back, t_three) * scale
        total = total + omegas[slot] * jnp.cos(omegas[slot] * saved) * back
    return total


def on_device(adjoint, saved, spectra, freq_index, picked):
    return plain_path(adjoint, saved, spectra, chosen_index(freq_index, picked))


def solution(mesh):
    placed = (
        P(("chain", "px"), "py", None),
        P(("chain", "px"), "py", None),
        P(None, None, "px", None),
        P(),
        P(),
    )
    return jax.shard_map(
        on_device,
        mesh=mesh,
        in_specs=placed,
        out_specs=P(("chain", "px"), "py", None),
        check_vma=False,
    )
```

```python
import functools
import math

import jax
import jax.numpy as jnp
import numpy as np
from jax import lax
from jax.experimental import pallas as pl
from jax.experimental.pallas import tpu as pltpu
from jax.sharding import PartitionSpec as P


def hartley(length):
    counter = np.arange(length, dtype=np.int64)
    angle = (counter[:, None] * counter[None, :] % length) * (2.0 * np.pi / length)
    return np.cos(angle) + np.sin(angle)


def chosen_index(freq_index, picked):
    ids = jnp.arange(freq_index.shape[0], dtype=jnp.int32)
    return jnp.sum(jnp.where(ids[None, :] == picked[:, None], freq_index[None, :], 0), axis=1)


def along(equation, field, table):
    return jnp.einsum(equation, field, jnp.asarray(table, jnp.float32), precision=lax.Precision.HIGH)


def plain_path(adjoint, saved, spectra, chosen):
    size_px, size_py = lax.axis_size("px"), lax.axis_size("py")
    one, two, three = adjoint.shape[0] * size_px, adjoint.shape[1] * size_py, adjoint.shape[2]
    t_one, t_two, t_three = hartley(one), hartley(two), hartley(three)
    width = three // size_py
    field = along("abc,cz->abz", adjoint, t_three)
    field = lax.all_to_all(field, "py", split_axis=2, concat_axis=1, tiled=True)
    field = along("abc,bz->azc", field, t_two)
    field = lax.all_to_all(field, "px", split_axis=1, concat_axis=0, tiled=True)
    spectrum = along("abc,az->zbc", field, t_one)
    kernels = lax.dynamic_slice_in_dim(spectra, lax.axis_index("py") * width, width, 3)
    omegas = chosen.astype(jnp.float32) * (math.pi / 8.0)
    scale = 1.0 / (one * two * three)
    total = jnp.zeros(saved.shape, jnp.float32)
    for slot in range(chosen.shape[0]):
        back = along("abc,az->zbc", spectrum * kernels[slot].astype(jnp.float32), t_one)
        back = lax.all_to_all(back, "px", split_axis=0, concat_axis=1, tiled=True)
        back = along("abc,bz->azc", back, t_two)
        back = lax.all_to_all(back, "py", split_axis=1, concat_axis=2, tiled=True)
        back = along("abc,cz->abz", back, t_three) * scale
        total = total + omegas[slot] * jnp.cos(omegas[slot] * saved) * back
    return total


def as_three(matrix, axis):
    high = matrix.astype(jnp.bfloat16)
    low = (matrix - high.astype(np.float64)).astype(jnp.bfloat16)
    order = (high, high, low)
    return jnp.asarray(np.concatenate(order, axis=axis))


def split(value, axis):
    high = value.astype(jnp.bfloat16)
    low = (value - high.astype(jnp.float32)).astype(jnp.bfloat16)
    return jnp.concatenate([high, low, high], axis=axis)


def from_right(rows, table):
    return jnp.dot(split(rows, 1), table, preferred_element_type=jnp.float32)


def from_left(table, columns):
    return jnp.dot(table, split(columns, 0), preferred_element_type=jnp.float32)


def params(**more):
    return pltpu.CompilerParams(vmem_limit_bytes=58 << 20, **more)


def third_kernel(field_ref, table_ref, out_ref):
    planes, lines, three = field_ref.shape
    parts, _, _, width = out_ref.shape
    result = from_right(field_ref[...].reshape(planes * lines, three), table_ref[...])
    for part in range(parts):
        piece = result[:, part * width : (part + 1) * width]
        out_ref[part] = piece.reshape(planes, lines, width)


def second_kernel(field_ref, table_ref, out_ref, held):
    parts, planes, _, width = field_ref.shape
    size_px, local, _, _ = out_ref.shape
    for plane in range(0, planes, 2):
        sides = [
            jnp.concatenate([field_ref[part, at] for part in range(parts)], axis=0)
            for at in (plane, plane + 1)
        ]
        result = from_left(table_ref[...], jnp.concatenate(sides, axis=1))
        held[plane] = result[:, :width]
        held[plane + 1] = result[:, width:]
    for peer in range(size_px):
        out_ref[peer] = jnp.swapaxes(held[:, peer * local : (peer + 1) * local, :], 0, 1)


def second_back_kernel(field_ref, table_ref, out_ref, held):
    _, size_px, local, planes, width = field_ref.shape
    parts, _, _, lines, _ = out_ref.shape
    for peer in range(size_px):
        held[:, peer * local : (peer + 1) * local, :] = jnp.swapaxes(field_ref[0, peer], 0, 1)
    for plane in range(0, planes, 2):
        columns = jnp.concatenate([held[plane], held[plane + 1]], axis=1)
        result = from_left(table_ref[...], columns)
        for part in range(parts):
            rows = result[part * lines : (part + 1) * lines]
            out_ref[part, 0, plane] = rows[:, :width]
            out_ref[part, 0, plane + 1] = rows[:, width:]


def cosine_turns(turns):
    turns = turns - jnp.floor(turns + 0.5)
    square = turns * turns * (4.0 * math.pi * math.pi)
    value = jnp.full_like(square, 1.0 / math.factorial(20))
    for order in range(9, -1, -1):
        value = value * square + (-1.0) ** order / math.factorial(2 * order)
    return value


def third_back_kernel(scale, chosen_ref, field_ref, saved_ref, table_ref, out_ref):
    parts, slots, planes, lines, width = field_ref.shape
    three = parts * width
    total = None
    site = saved_ref[...].reshape(planes * lines, three)
    for slot in range(slots):
        sides = [field_ref[part, slot].reshape(planes * lines, width) for part in range(parts)]
        field = from_right(jnp.concatenate(sides, axis=1), table_ref[...])
        index = chosen_ref[slot].astype(jnp.float32)
        weight = cosine_turns(site * (index * (1.0 / 16.0))) * (index * (math.pi / 8.0 * scale))
        total = weight * field if total is None else total + weight * field
    out_ref[...] = total.reshape(planes, lines, three)


def middle_kernel(
    chunks,
    field_ref,
    spectra_ref,
    table_ref,
    out_ref,
    gathered,
    raw,
    kernels,
    product,
    go_send,
    go_recv,
    back_send,
    back_recv,
    own_sem,
    back_own,
    raw_sem,
):
    size_px, local, planes, width = field_ref.shape
    slots, one = raw.shape[0], raw.shape[1]
    step = local // chunks
    me = lax.axis_index("px")
    part = lax.axis_index("py")

    def peer_of(turn):
        return lax.rem(me + turn, size_px)

    def go(chunk, sender, receiver):
        rows = pl.ds(chunk * step, step)
        return pltpu.make_async_remote_copy(
            src_ref=field_ref.at[receiver, rows],
            dst_ref=gathered.at[sender, rows],
            send_sem=go_send.at[chunk, receiver],
            recv_sem=go_recv.at[chunk, sender],
            device_id={"px": receiver},
            device_id_type=pl.DeviceIdType.MESH,
        )

    def back(slot, chunk, sender, receiver):
        rows = pl.ds(chunk * step, step)
        return pltpu.make_async_remote_copy(
            src_ref=product.at[slot, receiver, rows],
            dst_ref=out_ref.at[slot, sender, rows],
            send_sem=back_send.at[slot, chunk, receiver],
            recv_sem=back_recv.at[slot, chunk, sender],
            device_id={"px": receiver},
            device_id_type=pl.DeviceIdType.MESH,
        )

    own = pltpu.make_async_copy(field_ref.at[me], gathered.at[me], own_sem)
    fetch = pltpu.make_async_copy(spectra_ref.at[:, :, :, pl.ds(part * width, width)], raw, raw_sem)
    own.start()
    fetch.start()

    barrier = pltpu.get_barrier_semaphore()

    @pl.loop(1, size_px)
    def _(turn):
        pl.semaphore_signal(
            barrier, inc=1, device_id={"px": peer_of(turn)}, device_id_type=pl.DeviceIdType.MESH
        )

    pl.semaphore_wait(barrier, size_px - 1)

    @pl.loop(0, chunks)
    def _(chunk):
        @pl.loop(1, size_px)
        def _(turn):
            go(chunk, me, peer_of(turn)).start()

    own.wait()
    fetch.wait()
    block = 16

    @pl.loop(0, one // block)
    def _(at):
        rows = pl.ds(pl.multiple_of(at * block, block), block)
        for slot in range(slots):
            piece = raw[slot, rows].astype(jnp.float32)
            kernels[slot, :, rows, :] = jnp.swapaxes(piece, 0, 1)

    @pl.loop(0, chunks)
    def _(chunk):
        @pl.loop(1, size_px)
        def _(turn):
            go(chunk, peer_of(turn), me).wait_recv()

        @pl.loop(0, step // 2)
        def _(pair):
            first = chunk * step + pair * 2
            second = first + 1
            columns = jnp.concatenate(
                [gathered[:, at].reshape(one, width) for at in (first, second)], axis=1
            )
            spectrum = from_left(table_ref[...], columns)
            for slot in range(slots):
                factor = jnp.concatenate([kernels[slot, first], kernels[slot, second]], axis=1)
                result = from_left(table_ref[...], spectrum * factor)
                product[slot, :, first] = result[:, :width].reshape(size_px, planes, width)
                product[slot, :, second] = result[:, width:].reshape(size_px, planes, width)

        for slot in range(slots):

            @pl.loop(1, size_px)
            def _(turn):
                back(slot, chunk, me, peer_of(turn)).start()

    homes = [
        pltpu.make_async_copy(product.at[slot, me], out_ref.at[slot, me], back_own.at[slot])
        for slot in range(slots)
    ]
    for home in homes:
        home.start()

    @pl.loop(0, chunks)
    def _(chunk):
        @pl.loop(1, size_px)
        def _(turn):
            peer = peer_of(turn)
            go(chunk, me, peer).wait_send()
            for slot in range(slots):
                back(slot, chunk, me, peer).wait_send()
                back(slot, chunk, peer, me).wait_recv()

    for home in homes:
        home.wait()


def kernel_path(adjoint, saved, spectra, chosen):
    size_px, size_py = lax.axis_size("px"), lax.axis_size("py")
    planes, lines, three = adjoint.shape
    one, two = planes * size_px, lines * size_py
    width, local, slots = three // size_py, spectra.shape[2], chosen.shape[0]
    whole = lambda table: pl.BlockSpec(table.shape, lambda *at: (0,) * table.ndim)
    anywhere = pl.BlockSpec(memory_space=pl.ANY)
    f32 = jnp.float32
    block = 8
    right_three = as_three(hartley(three), 0)
    left_two, left_one = as_three(hartley(two), 1), as_three(hartley(one), 1)

    field = pl.pallas_call(
        third_kernel,
        grid=(planes // block,),
        in_specs=[pl.BlockSpec((block, lines, three), lambda i: (i, 0, 0)), whole(right_three)],
        out_specs=pl.BlockSpec((size_py, block, lines, width), lambda i: (0, i, 0, 0)),
        out_shape=jax.ShapeDtypeStruct((size_py, planes, lines, width), f32),
        compiler_params=params(),
        name="third",
    )(adjoint, right_three)
    field = lax.all_to_all(field, "py", split_axis=0, concat_axis=0, tiled=True)
    field = pl.pallas_call(
        second_kernel,
        grid=(planes // block,),
        in_specs=[
            pl.BlockSpec((size_py, block, lines, width), lambda i: (0, i, 0, 0)),
            whole(left_two),
        ],
        out_specs=pl.BlockSpec((size_px, local, block, width), lambda i: (0, 0, i, 0)),
        out_shape=jax.ShapeDtypeStruct((size_px, local, planes, width), f32),
        scratch_shapes=[pltpu.VMEM((block, two, width), f32)],
        compiler_params=params(),
        name="second",
    )(field, left_two)
    chunks = 4
    dma = pltpu.SemaphoreType.DMA
    field = pl.pallas_call(
        functools.partial(middle_kernel, chunks),
        in_specs=[anywhere, anywhere, pl.BlockSpec(memory_space=pltpu.VMEM)],
        out_specs=anywhere,
        out_shape=jax.ShapeDtypeStruct((slots, size_px, local, planes, width), f32),
        scratch_shapes=[
            pltpu.VMEM((size_px, local, planes, width), f32),
            pltpu.VMEM((slots, one, local, width), spectra.dtype),
            pltpu.VMEM((slots, local, one, width), f32),
            pltpu.VMEM((slots, size_px, local, planes, width), f32),
            dma((chunks, size_px)),
            dma((chunks, size_px)),
            dma((slots, chunks, size_px)),
            dma((slots, chunks, size_px)),
            dma,
            dma((slots,)),
            dma,
        ],
        compiler_params=params(collective_id=0, has_side_effects=True),
        name="middle",
    )(field, spectra, left_one)
    field = pl.pallas_call(
        second_back_kernel,
        grid=(slots, planes // block),
        in_specs=[
            pl.BlockSpec((1, size_px, local, block, width), lambda j, i: (j, 0, 0, i, 0)),
            whole(left_two),
        ],
        out_specs=pl.BlockSpec((size_py, 1, block, lines, width), lambda j, i: (0, j, i, 0, 0)),
        out_shape=jax.ShapeDtypeStruct((size_py, slots, planes, lines, width), f32),
        scratch_shapes=[pltpu.VMEM((block, two, width), f32)],
        compiler_params=params(),
        name="second_back",
    )(field, left_two)
    field = lax.all_to_all(field, "py", split_axis=0, concat_axis=0, tiled=True)
    scale = 1.0 / (one * two * three)
    piece = 4
    return pl.pallas_call(
        functools.partial(third_back_kernel, scale),
        grid=(planes // piece,),
        in_specs=[
            pl.BlockSpec(memory_space=pltpu.SMEM),
            pl.BlockSpec((size_py, slots, piece, lines, width), lambda i: (0, 0, i, 0, 0)),
            pl.BlockSpec((piece, lines, three), lambda i: (i, 0, 0)),
            whole(right_three),
        ],
        out_specs=pl.BlockSpec((piece, lines, three), lambda i: (i, 0, 0)),
        out_shape=jax.ShapeDtypeStruct((planes, lines, three), f32),
        compiler_params=params(),
        name="third_back",
    )(chosen, field, saved, right_three)


def on_device(adjoint, saved, spectra, freq_index, picked):
    chosen = chosen_index(freq_index, picked)
    width = adjoint.shape[2] // lax.axis_size("py")
    if adjoint.shape[0] % 8 == 0 and spectra.shape[2] % 8 == 0 and width % 128 == 0:
        return kernel_path(adjoint, saved, spectra, chosen)
    return plain_path(adjoint, saved, spectra, chosen)


def solution(mesh):
    placed = (
        P(("chain", "px"), "py", None),
        P(("chain", "px"), "py", None),
        P(None, None, "px", None),
        P(),
        P(),
    )
    return jax.shard_map(
        on_device,
        mesh=mesh,
        in_specs=placed,
        out_specs=P(("chain", "px"), "py", None),
        check_vma=False,
    )
```

```python
import functools
import math

import jax
import jax.numpy as jnp
import numpy as np
from jax import lax
from jax.experimental import pallas as pl
from jax.experimental.pallas import tpu as pltpu
from jax.sharding import PartitionSpec as P


def hartley(length):
    counter = np.arange(length, dtype=np.int64)
    angle = (counter[:, None] * counter[None, :] % length) * (2.0 * np.pi / length)
    return np.cos(angle) + np.sin(angle)


def chosen_index(freq_index, picked):
    ids = jnp.arange(freq_index.shape[0], dtype=jnp.int32)
    return jnp.sum(jnp.where(ids[None, :] == picked[:, None], freq_index[None, :], 0), axis=1)


def along(equation, field, table):
    return jnp.einsum(equation, field, jnp.asarray(table, jnp.float32), precision=lax.Precision.HIGH)


def plain_path(adjoint, saved, spectra, chosen):
    size_px, size_py = lax.axis_size("px"), lax.axis_size("py")
    one, two, three = adjoint.shape[0] * size_px, adjoint.shape[1] * size_py, adjoint.shape[2]
    t_one, t_two, t_three = hartley(one), hartley(two), hartley(three)
    width = three // size_py
    field = along("abc,cz->abz", adjoint, t_three)
    field = lax.all_to_all(field, "py", split_axis=2, concat_axis=1, tiled=True)
    field = along("abc,bz->azc", field, t_two)
    field = lax.all_to_all(field, "px", split_axis=1, concat_axis=0, tiled=True)
    spectrum = along("abc,az->zbc", field, t_one)
    kernels = lax.dynamic_slice_in_dim(spectra, lax.axis_index("py") * width, width, 3)
    omegas = chosen.astype(jnp.float32) * (math.pi / 8.0)
    scale = 1.0 / (one * two * three)
    total = jnp.zeros(saved.shape, jnp.float32)
    for slot in range(chosen.shape[0]):
        back = along("abc,az->zbc", spectrum * kernels[slot].astype(jnp.float32), t_one)
        back = lax.all_to_all(back, "px", split_axis=0, concat_axis=1, tiled=True)
        back = along("abc,bz->azc", back, t_two)
        back = lax.all_to_all(back, "py", split_axis=1, concat_axis=2, tiled=True)
        back = along("abc,cz->abz", back, t_three) * scale
        total = total + omegas[slot] * jnp.cos(omegas[slot] * saved) * back
    return total


def as_three(matrix, axis):
    high = matrix.astype(jnp.bfloat16)
    low = (matrix - high.astype(np.float64)).astype(jnp.bfloat16)
    order = (high, high, low)
    return jnp.asarray(np.concatenate(order, axis=axis))


def split(value, axis):
    high = value.astype(jnp.bfloat16)
    low = (value - high.astype(jnp.float32)).astype(jnp.bfloat16)
    return jnp.concatenate([high, low, high], axis=axis)


def from_right(rows, table):
    return jnp.dot(split(rows, 1), table, preferred_element_type=jnp.float32)


def from_left(table, columns):
    return jnp.dot(table, split(columns, 0), preferred_element_type=jnp.float32)


def params(**more):
    return pltpu.CompilerParams(vmem_limit_bytes=58 << 20, **more)


def third_kernel(field_ref, table_ref, out_ref):
    planes, lines, three = field_ref.shape
    parts, _, _, width = out_ref.shape
    result = from_right(field_ref[...].reshape(planes * lines, three), table_ref[...])
    for part in range(parts):
        piece = result[:, part * width : (part + 1) * width]
        out_ref[part] = piece.reshape(planes, lines, width)


def second_kernel(field_ref, table_ref, out_ref, held):
    parts, planes, _, width = field_ref.shape
    size_px, local, _, _ = out_ref.shape
    for plane in range(0, planes, 2):
        sides = [
            jnp.concatenate([field_ref[part, at] for part in range(parts)], axis=0)
            for at in (plane, plane + 1)
        ]
        result = from_left(table_ref[...], jnp.concatenate(sides, axis=1))
        held[plane] = result[:, :width]
        held[plane + 1] = result[:, width:]
    for peer in range(size_px):
        out_ref[peer] = jnp.swapaxes(held[:, peer * local : (peer + 1) * local, :], 0, 1)


def second_back_kernel(field_ref, table_ref, out_ref, held):
    _, size_px, local, planes, width = field_ref.shape
    parts, _, _, lines, _ = out_ref.shape
    for peer in range(size_px):
        held[:, peer * local : (peer + 1) * local, :] = jnp.swapaxes(field_ref[0, peer], 0, 1)
    for plane in range(0, planes, 2):
        columns = jnp.concatenate([held[plane], held[plane + 1]], axis=1)
        result = from_left(table_ref[...], columns)
        for part in range(parts):
            rows = result[part * lines : (part + 1) * lines]
            out_ref[part, 0, plane] = rows[:, :width]
            out_ref[part, 0, plane + 1] = rows[:, width:]


def cosine_turns(turns):
    turns = turns - jnp.floor(turns + 0.5)
    square = turns * turns * (4.0 * math.pi * math.pi)
    value = jnp.full_like(square, 1.0 / math.factorial(20))
    for order in range(9, -1, -1):
        value = value * square + (-1.0) ** order / math.factorial(2 * order)
    return value


def third_back_kernel(scale, chosen_ref, field_ref, saved_ref, table_ref, out_ref):
    parts, slots, planes, lines, width = field_ref.shape
    three = parts * width
    total = None
    site = saved_ref[...].reshape(planes * lines, three)
    for slot in range(slots):
        sides = [field_ref[part, slot].reshape(planes * lines, width) for part in range(parts)]
        field = from_right(jnp.concatenate(sides, axis=1), table_ref[...])
        index = chosen_ref[slot].astype(jnp.float32)
        weight = cosine_turns(site * (index * (1.0 / 16.0))) * (index * (math.pi / 8.0 * scale))
        total = weight * field if total is None else total + weight * field
    out_ref[...] = total.reshape(planes, lines, three)


def middle_kernel(
    chunks,
    field_ref,
    spectra_ref,
    table_ref,
    out_ref,
    gathered,
    raw,
    kernels,
    product,
    go_send,
    go_recv,
    back_send,
    back_recv,
    plane_send,
    plane_recv,
    own_sem,
    back_own,
    raw_sem,
):
    half, rows_all, planes, width = field_ref.shape
    size_px, local = 2 * half, rows_all // 2
    slots, one = raw.shape[0], raw.shape[1]
    step = local // chunks
    me = lax.axis_index("px")
    part = lax.axis_index("py")
    lower = me < half
    base = jnp.where(lower, 0, half)
    place = me - base

    def block_of(owner):
        return jnp.where(owner < half, owner, size_px - 1 - owner)

    def other(turn):
        return half - base + lax.rem(place + turn, half)

    def mate(turn):
        return base + lax.rem(place + turn, half)

    def to(index):
        return dict(device_id={"px": index}, device_id_type=pl.DeviceIdType.MESH)

    def go(chunk, sender, receiver):
        rows = pl.ds(chunk * 2 * step, 2 * step)
        return pltpu.make_async_remote_copy(
            src_ref=field_ref.at[block_of(receiver), rows],
            dst_ref=gathered.at[sender, rows],
            send_sem=go_send.at[chunk, receiver],
            recv_sem=go_recv.at[chunk, sender],
            **to(receiver),
        )

    def back(slot, chunk, sender, receiver):
        rows = pl.ds(chunk * 2 * step, 2 * step)
        return pltpu.make_async_remote_copy(
            src_ref=product.at[slot, receiver - base, rows],
            dst_ref=out_ref.at[slot, block_of(sender), rows],
            send_sem=back_send.at[slot, chunk, receiver - base],
            recv_sem=back_recv.at[slot, chunk, sender - base],
            **to(receiver),
        )

    def plane(kind, send, receiver):
        return pltpu.make_async_remote_copy(
            src_ref=kernels.at[:, 0],
            dst_ref=kernels.at[:, local + kind],
            send_sem=plane_send.at[send],
            recv_sem=plane_recv.at[kind],
            **to(receiver),
        )

    own = pltpu.make_async_copy(field_ref.at[block_of(me)], gathered.at[me], own_sem)
    fetch = pltpu.make_async_copy(spectra_ref.at[:, :, :, pl.ds(part * width, width)], raw, raw_sem)
    own.start()
    fetch.start()

    barrier = pltpu.get_barrier_semaphore()

    @pl.loop(1, size_px)
    def _(turn):
        pl.semaphore_signal(barrier, inc=1, **to(lax.rem(me + turn, size_px)))

    pl.semaphore_wait(barrier, size_px - 1)

    def send_chunk(at):
        chunk = chunks - 1 - at

        @pl.loop(0, half)
        def _(turn):
            go(chunk, me, other(turn)).start()

        @pl.loop(1, half)
        def _(turn):
            go(chunk, me, mate(turn)).start()

    early = chunks // 2
    pl.loop(0, early)(send_chunk)
    own.wait()
    fetch.wait()
    block = 16

    @pl.loop(0, one // block)
    def _(at):
        rows = pl.ds(pl.multiple_of(at * block, block), block)
        for slot in range(slots):
            piece = raw[slot, rows].astype(jnp.float32)
            kernels[slot, 0:local, rows, :] = jnp.swapaxes(piece, 0, 1)

    before = lax.rem(me + size_px - 1, size_px)
    ends = (me == 0) | (me == size_px - 1)

    @pl.when(before >= half)
    def _():
        plane(0, 0, before).start()

    @pl.when(me == half)
    def _():
        plane(1, 1, 0).start()
        plane(1, 2, size_px - 1).start()

    pl.loop(early, chunks)(send_chunk)

    @pl.loop(0, chunks)
    def _(at):
        chunk = chunks - 1 - at

        @pl.loop(0, half)
        def _(turn):
            go(chunk, other(turn), me).wait_recv()

        @pl.loop(1, half)
        def _(turn):
            go(chunk, mate(turn), me).wait_recv()

        @pl.when(chunk == 0)
        def _():
            @pl.when(jnp.logical_not(lower))
            def _():
                plane(0, 0, before).wait_recv()

            @pl.when(ends)
            def _():
                plane(1, 1, before).wait_recv()

        own_sites = pl.ds(pl.multiple_of(base * planes, half * planes), half * planes)

        @pl.loop(0, step)
        def _(inner):
            line = chunk * step + inner
            first, second = 2 * line, 2 * line + 1
            columns = jnp.concatenate(
                [gathered[:, at].reshape(one, width) for at in (first, second)], axis=1
            )
            spectrum = from_left(table_ref[...], columns)
            leading = line == 0
            plain = jnp.where(lower, line, local - line)
            mirrored = jnp.where(leading & ends, local + 1, plain)
            for slot in range(slots):
                factor = jnp.concatenate([kernels[slot, plain], kernels[slot, mirrored]], axis=1)
                result = from_left(table_ref[own_sites, :], spectrum * factor)
                product[slot, :, first] = result[:, :width].reshape(half, planes, width)
                product[slot, :, second] = result[:, width:].reshape(half, planes, width)

        for slot in range(slots):

            @pl.loop(1, half)
            def _(turn):
                back(slot, chunk, me, mate(turn)).start()

    homes = [
        pltpu.make_async_copy(
            product.at[slot, place], out_ref.at[slot, block_of(me)], back_own.at[slot]
        )
        for slot in range(slots)
    ]
    for home in homes:
        home.start()

    @pl.loop(0, chunks)
    def _(chunk):
        @pl.loop(1, size_px)
        def _(turn):
            go(chunk, me, lax.rem(me + turn, size_px)).wait_send()

        @pl.loop(1, half)
        def _(turn):
            for slot in range(slots):
                back(slot, chunk, me, mate(turn)).wait_send()
                back(slot, chunk, mate(turn), me).wait_recv()

    @pl.when(before >= half)
    def _():
        plane(0, 0, before).wait_send()

    @pl.when(me == half)
    def _():
        plane(1, 1, 0).wait_send()
        plane(1, 2, size_px - 1).wait_send()

    for home in homes:
        home.wait()


def paired_order(length):
    counter = np.arange(length // 2)
    mirror = np.where(counter == 0, length // 2, length - counter)
    return np.stack([counter, mirror], axis=1).reshape(-1)


def kernel_path(adjoint, saved, spectra, chosen):
    size_px, size_py = lax.axis_size("px"), lax.axis_size("py")
    planes, lines, three = adjoint.shape
    one, two = planes * size_px, lines * size_py
    width, local, slots = three // size_py, spectra.shape[2], chosen.shape[0]
    whole = lambda table: pl.BlockSpec(table.shape, lambda *at: (0,) * table.ndim)
    anywhere = pl.BlockSpec(memory_space=pl.ANY)
    f32 = jnp.float32
    block = 8
    right_three = as_three(hartley(three), 0)
    order, half = paired_order(two), size_px // 2
    left_two = as_three(hartley(two)[order], 1)
    left_two_back = as_three(hartley(two)[:, order], 1)
    left_one = as_three(hartley(one), 1)

    field = pl.pallas_call(
        third_kernel,
        grid=(planes // block,),
        in_specs=[pl.BlockSpec((block, lines, three), lambda i: (i, 0, 0)), whole(right_three)],
        out_specs=pl.BlockSpec((size_py, block, lines, width), lambda i: (0, i, 0, 0)),
        out_shape=jax.ShapeDtypeStruct((size_py, planes, lines, width), f32),
        compiler_params=params(),
        name="third",
    )(adjoint, right_three)
    field = lax.all_to_all(field, "py", split_axis=0, concat_axis=0, tiled=True)
    field = pl.pallas_call(
        second_kernel,
        grid=(planes // block,),
        in_specs=[
            pl.BlockSpec((size_py, block, lines, width), lambda i: (0, i, 0, 0)),
            whole(left_two),
        ],
        out_specs=pl.BlockSpec((half, 2 * local, block, width), lambda i: (0, 0, i, 0)),
        out_shape=jax.ShapeDtypeStruct((half, 2 * local, planes, width), f32),
        scratch_shapes=[pltpu.VMEM((block, two, width), f32)],
        compiler_params=params(),
        name="second",
    )(field, left_two)
    chunks = 8
    dma = pltpu.SemaphoreType.DMA
    field = pl.pallas_call(
        functools.partial(middle_kernel, chunks),
        in_specs=[anywhere, anywhere, pl.BlockSpec(memory_space=pltpu.VMEM)],
        out_specs=anywhere,
        out_shape=jax.ShapeDtypeStruct((slots, half, 2 * local, planes, width), f32),
        scratch_shapes=[
            pltpu.VMEM((size_px, 2 * local, planes, width), f32),
            pltpu.VMEM((slots, one, local, width), spectra.dtype),
            pltpu.VMEM((slots, local + 2, one, width), f32),
            pltpu.VMEM((slots, half, 2 * local, planes, width), f32),
            dma((chunks, size_px)),
            dma((chunks, size_px)),
            dma((slots, chunks, half)),
            dma((slots, chunks, half)),
            dma((3,)),
            dma((2,)),
            dma,
            dma((slots,)),
            dma,
        ],
        compiler_params=params(collective_id=0, has_side_effects=True),
        name="middle",
    )(field, spectra, left_one)
    field = pl.pallas_call(
        second_back_kernel,
        grid=(slots, planes // block),
        in_specs=[
            pl.BlockSpec((1, half, 2 * local, block, width), lambda j, i: (j, 0, 0, i, 0)),
            whole(left_two_back),
        ],
        out_specs=pl.BlockSpec((size_py, 1, block, lines, width), lambda j, i: (0, j, i, 0, 0)),
        out_shape=jax.ShapeDtypeStruct((size_py, slots, planes, lines, width), f32),
        scratch_shapes=[pltpu.VMEM((block, two, width), f32)],
        compiler_params=params(),
        name="second_back",
    )(field, left_two_back)
    field = lax.all_to_all(field, "py", split_axis=0, concat_axis=0, tiled=True)
    scale = 1.0 / (one * two * three)
    piece = 4
    return pl.pallas_call(
        functools.partial(third_back_kernel, scale),
        grid=(planes // piece,),
        in_specs=[
            pl.BlockSpec(memory_space=pltpu.SMEM),
            pl.BlockSpec((size_py, slots, piece, lines, width), lambda i: (0, 0, i, 0, 0)),
            pl.BlockSpec((piece, lines, three), lambda i: (i, 0, 0)),
            whole(right_three),
        ],
        out_specs=pl.BlockSpec((piece, lines, three), lambda i: (i, 0, 0)),
        out_shape=jax.ShapeDtypeStruct((planes, lines, three), f32),
        compiler_params=params(),
        name="third_back",
    )(chosen, field, saved, right_three)


def on_device(adjoint, saved, spectra, freq_index, picked):
    chosen = chosen_index(freq_index, picked)
    width = adjoint.shape[2] // lax.axis_size("py")
    even = lax.axis_size("px") % 2 == 0
    if even and adjoint.shape[0] % 8 == 0 and spectra.shape[2] % 8 == 0 and width % 128 == 0:
        return kernel_path(adjoint, saved, spectra, chosen)
    return plain_path(adjoint, saved, spectra, chosen)


def solution(mesh):
    placed = (
        P(("chain", "px"), "py", None),
        P(("chain", "px"), "py", None),
        P(None, None, "px", None),
        P(),
        P(),
    )
    return jax.shard_map(
        on_device,
        mesh=mesh,
        in_specs=placed,
        out_specs=P(("chain", "px"), "py", None),
        check_vma=False,
    )
```

```python
import functools
import math

import jax
import jax.numpy as jnp
import numpy as np
from jax import lax
from jax.experimental import pallas as pl
from jax.experimental.pallas import tpu as pltpu
from jax.sharding import PartitionSpec as P


def hartley(length):
    counter = np.arange(length, dtype=np.int64)
    angle = (counter[:, None] * counter[None, :] % length) * (2.0 * np.pi / length)
    return np.cos(angle) + np.sin(angle)


def chosen_index(freq_index, picked):
    ids = jnp.arange(freq_index.shape[0], dtype=jnp.int32)
    return jnp.sum(jnp.where(ids[None, :] == picked[:, None], freq_index[None, :], 0), axis=1)


def along(equation, field, table):
    return jnp.einsum(equation, field, jnp.asarray(table, jnp.float32), precision=lax.Precision.HIGH)


def plain_path(adjoint, saved, spectra, chosen):
    size_px, size_py = lax.axis_size("px"), lax.axis_size("py")
    one, two, three = adjoint.shape[0] * size_px, adjoint.shape[1] * size_py, adjoint.shape[2]
    t_one, t_two, t_three = hartley(one), hartley(two), hartley(three)
    width = three // size_py
    field = along("abc,cz->abz", adjoint, t_three)
    field = lax.all_to_all(field, "py", split_axis=2, concat_axis=1, tiled=True)
    field = along("abc,bz->azc", field, t_two)
    field = lax.all_to_all(field, "px", split_axis=1, concat_axis=0, tiled=True)
    spectrum = along("abc,az->zbc", field, t_one)
    kernels = lax.dynamic_slice_in_dim(spectra, lax.axis_index("py") * width, width, 3)
    omegas = chosen.astype(jnp.float32) * (math.pi / 8.0)
    scale = 1.0 / (one * two * three)
    total = jnp.zeros(saved.shape, jnp.float32)
    for slot in range(chosen.shape[0]):
        back = along("abc,az->zbc", spectrum * kernels[slot].astype(jnp.float32), t_one)
        back = lax.all_to_all(back, "px", split_axis=0, concat_axis=1, tiled=True)
        back = along("abc,bz->azc", back, t_two)
        back = lax.all_to_all(back, "py", split_axis=1, concat_axis=2, tiled=True)
        back = along("abc,cz->abz", back, t_three) * scale
        total = total + omegas[slot] * jnp.cos(omegas[slot] * saved) * back
    return total


def as_three(matrix, axis):
    high = matrix.astype(jnp.bfloat16)
    low = (matrix - high.astype(np.float64)).astype(jnp.bfloat16)
    order = (high, high, low)
    return jnp.asarray(np.concatenate(order, axis=axis))


def split(value, axis):
    high = value.astype(jnp.bfloat16)
    low = (value - high.astype(jnp.float32)).astype(jnp.bfloat16)
    return jnp.concatenate([high, low, high], axis=axis)


def from_right(rows, table):
    return jnp.dot(split(rows, 1), table, preferred_element_type=jnp.float32)


def from_left(table, columns):
    return jnp.dot(table, split(columns, 0), preferred_element_type=jnp.float32)


def params(**more):
    return pltpu.CompilerParams(vmem_limit_bytes=58 << 20, **more)


def core_exchange(step, steps, source, target, sems):
    send_sem, recv_sem, own_sem = sems
    me = lax.axis_index("py")
    other = 1 - me

    def away(at, sender, receiver):
        return pltpu.make_async_remote_copy(
            src_ref=source(receiver, at),
            dst_ref=target(sender, at),
            send_sem=send_sem.at[at],
            recv_sem=recv_sem.at[at],
            device_id={"py": receiver},
            device_id_type=pl.DeviceIdType.MESH,
        )

    def stay(at):
        return pltpu.make_async_copy(source(me, at), target(me, at), own_sem.at[at])

    away(step, me, other).start()
    stay(step).start()

    @pl.when(step == steps - 1)
    def _():
        @pl.loop(0, steps)
        def _(at):
            away(at, me, other).wait_send()
            away(at, other, me).wait_recv()
            stay(at).wait()


def greet_core():
    barrier = pltpu.get_barrier_semaphore()
    other = 1 - lax.axis_index("py")
    pl.semaphore_signal(
        barrier, inc=1, device_id={"py": other}, device_id_type=pl.DeviceIdType.MESH
    )
    pl.semaphore_wait(barrier, 1)


def third_kernel(steps, field_ref, table_ref, out_ref, mine, *sems):
    planes, lines, three = field_ref.shape
    parts, width = mine.shape[0], mine.shape[3]
    step = pl.program_id(0)
    pl.when(step == 0)(greet_core)

    def rows(at):
        return pl.ds(pl.multiple_of(at * planes, planes), planes)

    result = from_right(field_ref[...].reshape(planes * lines, three), table_ref[...])
    for part in range(parts):
        piece = result[:, part * width : (part + 1) * width]
        mine[part, rows(step)] = piece.reshape(planes, lines, width)
    core_exchange(
        step,
        steps,
        lambda part, at: mine.at[part, rows(at)],
        lambda part, at: out_ref.at[part, rows(at)],
        sems,
    )


def second_kernel(field_ref, table_ref, out_ref, held):
    parts, planes, _, width = field_ref.shape
    size_px, local, _, _ = out_ref.shape
    for plane in range(0, planes, 2):
        sides = [
            jnp.concatenate([field_ref[part, at] for part in range(parts)], axis=0)
            for at in (plane, plane + 1)
        ]
        result = from_left(table_ref[...], jnp.concatenate(sides, axis=1))
        held[plane] = result[:, :width]
        held[plane + 1] = result[:, width:]
    for peer in range(size_px):
        out_ref[peer] = jnp.swapaxes(held[:, peer * local : (peer + 1) * local, :], 0, 1)


def second_back_kernel(steps, field_ref, table_ref, out_ref, held, mine, *sems):
    _, groups, local, planes, width = field_ref.shape
    parts, lines = mine.shape[0], mine.shape[3]
    inner = steps // mine.shape[1]
    step = pl.program_id(0) * inner + pl.program_id(1)
    slot = pl.program_id(0)
    begin = pl.program_id(1) * planes
    pl.when(step == 0)(greet_core)
    for group in range(groups):
        held[:, group * local : (group + 1) * local, :] = jnp.swapaxes(field_ref[0, group], 0, 1)
    for plane in range(0, planes, 2):
        columns = jnp.concatenate([held[plane], held[plane + 1]], axis=1)
        result = from_left(table_ref[...], columns)
        for part in range(parts):
            rows = result[part * lines : (part + 1) * lines]
            mine[part, slot, begin + plane] = rows[:, :width]
            mine[part, slot, begin + plane + 1] = rows[:, width:]

    def block(ref):
        return lambda part, at: ref.at[part, at // inner, pl.ds((at % inner) * planes, planes)]

    core_exchange(step, steps, block(mine), block(out_ref), sems)


def cosine_turns(turns):
    turns = turns - jnp.floor(turns + 0.5)
    square = turns * turns * (4.0 * math.pi * math.pi)
    value = jnp.full_like(square, 1.0 / math.factorial(20))
    for order in range(9, -1, -1):
        value = value * square + (-1.0) ** order / math.factorial(2 * order)
    return value


def third_back_kernel(scale, chosen_ref, field_ref, saved_ref, table_ref, out_ref):
    parts, slots, planes, lines, width = field_ref.shape
    three = parts * width
    total = None
    site = saved_ref[...].reshape(planes * lines, three)
    for slot in range(slots):
        sides = [field_ref[part, slot].reshape(planes * lines, width) for part in range(parts)]
        field = from_right(jnp.concatenate(sides, axis=1), table_ref[...])
        index = chosen_ref[slot].astype(jnp.float32)
        weight = cosine_turns(site * (index * (1.0 / 16.0))) * (index * (math.pi / 8.0 * scale))
        total = weight * field if total is None else total + weight * field
    out_ref[...] = total.reshape(planes, lines, three)


def middle_kernel(
    chunks,
    field_ref,
    spectra_ref,
    table_ref,
    out_ref,
    gathered,
    raw,
    kernels,
    product,
    go_send,
    go_recv,
    back_send,
    back_recv,
    plane_send,
    plane_recv,
    own_sem,
    back_own,
    raw_sem,
):
    half, rows_all, planes, width = field_ref.shape
    size_px, local = 2 * half, rows_all // 2
    slots, one = raw.shape[0], raw.shape[1]
    step = local // chunks
    me = lax.axis_index("px")
    part = lax.axis_index("py")
    lower = me < half
    base = jnp.where(lower, 0, half)
    place = me - base

    def block_of(owner):
        return jnp.where(owner < half, owner, size_px - 1 - owner)

    def other(turn):
        return half - base + lax.rem(place + turn, half)

    def mate(turn):
        return base + lax.rem(place + turn, half)

    def to(index):
        return dict(device_id={"px": index}, device_id_type=pl.DeviceIdType.MESH)

    def go(chunk, sender, receiver):
        rows = pl.ds(chunk * 2 * step, 2 * step)
        return pltpu.make_async_remote_copy(
            src_ref=field_ref.at[block_of(receiver), rows],
            dst_ref=gathered.at[sender, rows],
            send_sem=go_send.at[chunk, receiver],
            recv_sem=go_recv.at[chunk, sender],
            **to(receiver),
        )

    def back(slot, chunk, sender, receiver):
        rows = pl.ds(chunk * 2 * step, 2 * step)
        return pltpu.make_async_remote_copy(
            src_ref=product.at[slot, receiver - base, rows],
            dst_ref=out_ref.at[slot, block_of(sender), rows],
            send_sem=back_send.at[slot, chunk, receiver - base],
            recv_sem=back_recv.at[slot, chunk, sender - base],
            **to(receiver),
        )

    def plane(kind, send, receiver):
        return pltpu.make_async_remote_copy(
            src_ref=kernels.at[:, 0],
            dst_ref=kernels.at[:, local + kind],
            send_sem=plane_send.at[send],
            recv_sem=plane_recv.at[kind],
            **to(receiver),
        )

    own = pltpu.make_async_copy(field_ref.at[block_of(me)], gathered.at[me], own_sem)
    fetch = pltpu.make_async_copy(spectra_ref.at[:, :, :, pl.ds(part * width, width)], raw, raw_sem)
    own.start()
    fetch.start()

    barrier = pltpu.get_barrier_semaphore()

    @pl.loop(1, size_px)
    def _(turn):
        pl.semaphore_signal(barrier, inc=1, **to(lax.rem(me + turn, size_px)))

    pl.semaphore_wait(barrier, size_px - 1)

    def send_chunk(at):
        chunk = chunks - 1 - at

        @pl.loop(0, half)
        def _(turn):
            go(chunk, me, other(turn)).start()

        @pl.loop(1, half)
        def _(turn):
            go(chunk, me, mate(turn)).start()

    early = chunks // 2
    pl.loop(0, early)(send_chunk)
    own.wait()
    fetch.wait()
    block = 16

    @pl.loop(0, one // block)
    def _(at):
        rows = pl.ds(pl.multiple_of(at * block, block), block)
        for slot in range(slots):
            piece = raw[slot, rows].astype(jnp.float32)
            kernels[slot, 0:local, rows, :] = jnp.swapaxes(piece, 0, 1)

    before = lax.rem(me + size_px - 1, size_px)
    ends = (me == 0) | (me == size_px - 1)

    @pl.when(before >= half)
    def _():
        plane(0, 0, before).start()

    @pl.when(me == half)
    def _():
        plane(1, 1, 0).start()
        plane(1, 2, size_px - 1).start()

    pl.loop(early, chunks)(send_chunk)

    @pl.loop(0, chunks)
    def _(at):
        chunk = chunks - 1 - at

        @pl.loop(0, half)
        def _(turn):
            go(chunk, other(turn), me).wait_recv()

        @pl.loop(1, half)
        def _(turn):
            go(chunk, mate(turn), me).wait_recv()

        @pl.when(chunk == 0)
        def _():
            @pl.when(jnp.logical_not(lower))
            def _():
                plane(0, 0, before).wait_recv()

            @pl.when(ends)
            def _():
                plane(1, 1, before).wait_recv()

        own_sites = pl.ds(pl.multiple_of(base * planes, half * planes), half * planes)

        @pl.loop(0, step)
        def _(inner):
            line = chunk * step + inner
            first, second = 2 * line, 2 * line + 1
            columns = jnp.concatenate(
                [gathered[:, at].reshape(one, width) for at in (first, second)], axis=1
            )
            spectrum = from_left(table_ref[...], columns)
            leading = line == 0
            plain = jnp.where(lower, line, local - line)
            mirrored = jnp.where(leading & ends, local + 1, plain)
            for slot in range(slots):
                factor = jnp.concatenate([kernels[slot, plain], kernels[slot, mirrored]], axis=1)
                result = from_left(table_ref[own_sites, :], spectrum * factor)
                product[slot, :, first] = result[:, :width].reshape(half, planes, width)
                product[slot, :, second] = result[:, width:].reshape(half, planes, width)

        for slot in range(slots):

            @pl.loop(1, half)
            def _(turn):
                back(slot, chunk, me, mate(turn)).start()

    homes = [
        pltpu.make_async_copy(
            product.at[slot, place], out_ref.at[slot, block_of(me)], back_own.at[slot]
        )
        for slot in range(slots)
    ]
    for home in homes:
        home.start()

    @pl.loop(0, chunks)
    def _(chunk):
        @pl.loop(1, size_px)
        def _(turn):
            go(chunk, me, lax.rem(me + turn, size_px)).wait_send()

        @pl.loop(1, half)
        def _(turn):
            for slot in range(slots):
                back(slot, chunk, me, mate(turn)).wait_send()
                back(slot, chunk, mate(turn), me).wait_recv()

    @pl.when(before >= half)
    def _():
        plane(0, 0, before).wait_send()

    @pl.when(me == half)
    def _():
        plane(1, 1, 0).wait_send()
        plane(1, 2, size_px - 1).wait_send()

    for home in homes:
        home.wait()


def paired_order(length):
    counter = np.arange(length // 2)
    mirror = np.where(counter == 0, length // 2, length - counter)
    return np.stack([counter, mirror], axis=1).reshape(-1)


def kernel_path(adjoint, saved, spectra, chosen):
    size_px, size_py = lax.axis_size("px"), lax.axis_size("py")
    planes, lines, three = adjoint.shape
    one, two = planes * size_px, lines * size_py
    width, local, slots = three // size_py, spectra.shape[2], chosen.shape[0]
    whole = lambda table: pl.BlockSpec(table.shape, lambda *at: (0,) * table.ndim)
    anywhere = pl.BlockSpec(memory_space=pl.ANY)
    f32 = jnp.float32
    block = 8
    steps = planes // block
    dma = pltpu.SemaphoreType.DMA
    right_three = as_three(hartley(three), 0)
    order, half = paired_order(two), size_px // 2
    left_two = as_three(hartley(two)[order], 1)
    left_two_back = as_three(hartley(two)[:, order], 1)
    left_one = as_three(hartley(one), 1)

    field = pl.pallas_call(
        functools.partial(third_kernel, steps),
        grid=(steps,),
        in_specs=[pl.BlockSpec((block, lines, three), lambda i: (i, 0, 0)), whole(right_three)],
        out_specs=anywhere,
        out_shape=jax.ShapeDtypeStruct((size_py, planes, lines, width), f32),
        scratch_shapes=[pltpu.VMEM((size_py, planes, lines, width), f32)] + [dma((steps,))] * 3,
        compiler_params=params(collective_id=1, has_side_effects=True),
        name="third",
    )(adjoint, right_three)
    field = pl.pallas_call(
        second_kernel,
        grid=(planes // block,),
        in_specs=[
            pl.BlockSpec((size_py, block, lines, width), lambda i: (0, i, 0, 0)),
            whole(left_two),
        ],
        out_specs=pl.BlockSpec((half, 2 * local, block, width), lambda i: (0, 0, i, 0)),
        out_shape=jax.ShapeDtypeStruct((half, 2 * local, planes, width), f32),
        scratch_shapes=[pltpu.VMEM((block, two, width), f32)],
        compiler_params=params(),
        name="second",
    )(field, left_two)
    chunks = 8
    field = pl.pallas_call(
        functools.partial(middle_kernel, chunks),
        in_specs=[anywhere, anywhere, pl.BlockSpec(memory_space=pltpu.VMEM)],
        out_specs=anywhere,
        out_shape=jax.ShapeDtypeStruct((slots, half, 2 * local, planes, width), f32),
        scratch_shapes=[
            pltpu.VMEM((size_px, 2 * local, planes, width), f32),
            pltpu.VMEM((slots, one, local, width), spectra.dtype),
            pltpu.VMEM((slots, local + 2, one, width), f32),
            pltpu.VMEM((slots, half, 2 * local, planes, width), f32),
            dma((chunks, size_px)),
            dma((chunks, size_px)),
            dma((slots, chunks, half)),
            dma((slots, chunks, half)),
            dma((3,)),
            dma((2,)),
            dma,
            dma((slots,)),
            dma,
        ],
        compiler_params=params(collective_id=0, has_side_effects=True),
        name="middle",
    )(field, spectra, left_one)
    field = pl.pallas_call(
        functools.partial(second_back_kernel, slots * steps),
        grid=(slots, steps),
        in_specs=[
            pl.BlockSpec((1, half, 2 * local, block, width), lambda j, i: (j, 0, 0, i, 0)),
            whole(left_two_back),
        ],
        out_specs=anywhere,
        out_shape=jax.ShapeDtypeStruct((size_py, slots, planes, lines, width), f32),
        scratch_shapes=[
            pltpu.VMEM((block, two, width), f32),
            pltpu.VMEM((size_py, slots, planes, lines, width), f32),
        ]
        + [dma((slots * steps,))] * 3,
        compiler_params=params(collective_id=2, has_side_effects=True),
        name="second_back",
    )(field, left_two_back)
    scale = 1.0 / (one * two * three)
    piece = 4
    return pl.pallas_call(
        functools.partial(third_back_kernel, scale),
        grid=(planes // piece,),
        in_specs=[
            pl.BlockSpec(memory_space=pltpu.SMEM),
            pl.BlockSpec((size_py, slots, piece, lines, width), lambda i: (0, 0, i, 0, 0)),
            pl.BlockSpec((piece, lines, three), lambda i: (i, 0, 0)),
            whole(right_three),
        ],
        out_specs=pl.BlockSpec((piece, lines, three), lambda i: (i, 0, 0)),
        out_shape=jax.ShapeDtypeStruct((planes, lines, three), f32),
        compiler_params=params(),
        name="third_back",
    )(chosen, field, saved, right_three)


def on_device(adjoint, saved, spectra, freq_index, picked):
    chosen = chosen_index(freq_index, picked)
    width = adjoint.shape[2] // lax.axis_size("py")
    even = lax.axis_size("px") % 2 == 0 and lax.axis_size("py") == 2
    if even and adjoint.shape[0] % 8 == 0 and spectra.shape[2] % 8 == 0 and width % 128 == 0:
        return kernel_path(adjoint, saved, spectra, chosen)
    return plain_path(adjoint, saved, spectra, chosen)


def solution(mesh):
    placed = (
        P(("chain", "px"), "py", None),
        P(("chain", "px"), "py", None),
        P(None, None, "px", None),
        P(),
        P(),
    )
    return jax.shard_map(
        on_device,
        mesh=mesh,
        in_specs=placed,
        out_specs=P(("chain", "px"), "py", None),
        check_vma=False,
    )
```
